512 devices in a mesh: sector: 16 (over y, x_lo, core), dom: 32 (over z, x_hi).
Axes of the slice: x: 4 (x_hi: 2, x_lo: 2; x = x_hi * 2 + x_lo), y: 4, z: 16, core: 2. Of those that a mesh axis runs over, the one named last changes fastest.
Arguments:
- amplitudes: float32 [64, 48], replicated, may hold values from -0.3 to 0.3
- mode_shapes: float32 [48, 3, 524288], P(None, None, ('sector', 'dom')), may hold values from -6 to 6
- shape_grads: float32 [8, 3, 524288], P(None, None, ('sector', 'dom')), may hold values from -2.4 to 2.4
- lame_params: float32 [2, 524288], P(None, ('sector', 'dom')), may hold values from 0.5 to 2
- connectivity: int32 [8, 524288], P(None, ('sector', 'dom')), may hold values from -1 to 1791, as said below
- dom_sends: int32 [2, 131072], P(None, ('sector', 'dom')), may hold values from -1 to 1023, as said below
- sector_sends: int32 [2, 65536], P(None, ('sector', 'dom')), may hold values from -1 to 1023, as said below
Outputs:
- nodal_force: float32 [64, 3, 524288], P(None, None, ('sector', 'dom'))
- modal_force: float32 [64, 48], replicated
The draws below stay inside these ranges and needn't reach their ends.
Inputs may be any that keep to these rules, and one draw needn't show every extreme that they name: `connectivity`: in each device's block, the live elements come first and the padding element slots after them hold -1 in all 8 rows; a live slot names a slot of the device's extended table. Some device has all 1024 slots live. `dom_sends`: each device's row lists its own node numbers first, then -1; a row holds 128 to 256 live entries, and some row is full. `sector_sends`: each device's row lists its own node numbers first, then -1; a row holds 64 to 128 live entries, and some row is full.
All inputs are finite; a program needn't handle non-finite values.
Results may differ from the reference program's by a relative error of at most 0.0003.
Values sent between devices are 32-bit elements; how exact they have to be, the bound alone decides.
A program may use at most 64 MiB of HBM per device.

```python
import math
import jax
import jax.numpy as jnp
from jax import lax

COMBOS = 64
MODES = 48
NODE_DEV = 1024
ELEM_DEV = 1024
IF_DOM = 256
IF_SEC = 128
EXT_NODES = 1792
NODES = 524288
ELEMENTS = 524288
N_SECTOR = 16
N_DOM = 32


def padded_lists(key, list_width):
    device_total = NODES // NODE_DEV
    key_live, key_full, key_nodes = jax.random.split(key, 3)
    live_slots = jax.random.randint(key_live, (2 * device_total,), list_width // 2, list_width + 1)
    chosen = jax.random.randint(key_full, (), 0, 2 * device_total)
    live_slots = jnp.where(jnp.arange(2 * device_total) == chosen, list_width, live_slots).reshape(2, device_total)
    picked = jax.random.randint(key_nodes, (2, device_total, list_width), 0, NODE_DEV)
    positions = jnp.arange(list_width)[None, None, :]
    lists_out = jnp.where(positions < live_slots[:, :, None], picked, -1)
    return lists_out.reshape(2, device_total * list_width).astype(jnp.int32)


def draw_dom_sends(key, part):
    return padded_lists(jax.random.fold_in(key, 11), IF_DOM)


def draw_sector_sends(key, part):
    return padded_lists(jax.random.fold_in(key, 23), IF_SEC)


def draw_connectivity(key, part):
    device_total = ELEMENTS // ELEM_DEV
    key_load, key_full, key_own, key_halo, key_pick = jax.random.split(jax.random.fold_in(key, 37), 5)
    loads = ELEM_DEV * 7 // 8 + ELEM_DEV // 32 * jax.random.randint(key_load, (device_total,), 0, 5)
    chosen = jax.random.randint(key_full, (), 0, device_total)
    loads = jnp.where(jnp.arange(device_total) == chosen, ELEM_DEV, loads)
    own_refs = jax.random.randint(key_own, (8, device_total, ELEM_DEV), 0, NODE_DEV)
    halo_refs = jax.random.randint(key_halo, (8, device_total, ELEM_DEV), NODE_DEV, EXT_NODES)
    picks = jax.random.randint(key_pick, (8, device_total, ELEM_DEV), 0, 5)
    refs = jnp.where(picks == 0, halo_refs, own_refs)
    live_mask = jnp.arange(ELEM_DEV)[None, None, :] < loads[None, :, None]
    return jnp.where(live_mask, refs, -1).reshape(8, ELEMENTS).astype(jnp.int32)


def level_of(own_key, shape, cuts, least, largest):
    def one(position, parts):
        draws = jax.random.uniform(jax.random.fold_in(jax.random.fold_in(own_key, 6), position), (parts,), jnp.float32, least / len(cuts), largest / len(cuts))
        return jnp.repeat(jnp.exp(draws), shape[position] // parts).reshape((-1,) + (1,) * (len(shape) - position - 1))

    level = one(*cuts[0])
    for cut in cuts[1:]:
        level = level * one(*cut)
    return level


def normal_values(own_key, extent, deviation, reach, shards=(), held_as=jnp.bfloat16):
    gain = level_of(own_key, extent, shards, -0.22, 0.18) if shards else 1.0
    values = jax.random.normal(own_key, extent, jnp.float32) * deviation * gain
    return jnp.minimum(jnp.maximum(values, -reach), reach).astype(held_as)


def setup_inputs(seed: int = 0) -> dict:
    key_list = jax.random.split(jax.random.key(seed), 8)
    return {
        "amplitudes": normal_values(key_list[0], (COMBOS, MODES), 0.05, 0.3, (), jnp.float32),
        "mode_shapes": normal_values(key_list[1], (MODES, 3, NODES), 1.0, 6.0, ((2, 512),), jnp.float32),
        "shape_grads": normal_values(key_list[2], (8, 3, ELEMENTS), 0.4, 2.4, ((2, 512),), jnp.float32),
        "lame_params": jnp.clip(jnp.exp(math.log(2.0) - 1.3862944 * jax.random.uniform(key_list[3], (2, ELEMENTS), jnp.float32) ** level_of(key_list[3], (2, ELEMENTS), ((1, 512),), -0.2, 0.2)), 0.5, 2.0),
        "connectivity": draw_connectivity(jax.random.fold_in(key_list[7], 71), 0),
        "dom_sends": draw_dom_sends(jax.random.fold_in(key_list[7], 71), 0),
        "sector_sends": draw_sector_sends(jax.random.fold_in(key_list[7], 71), 0),
    }


def take_slots(node_table, send_lists):
    slot_width = node_table.shape[1]
    slot_index = jnp.where(send_lists < 0, slot_width, send_lists).reshape(-1)
    return jnp.take(node_table, slot_index, axis=1, mode='fill', fill_value=0.0)

def add_slots(node_table, send_lists, add_values):
    slot_width = node_table.shape[1]
    slot_index = jnp.where(send_lists < 0, slot_width, send_lists).reshape(-1)
    return node_table.at[:, slot_index].add(add_values, mode='drop')

def element_forces(accum, extended, connect, gradients, lame):
    ext_width = extended.shape[1]
    combo_total = extended.shape[0] // 3
    elem_total = connect.shape[1]
    slot_index = jnp.where(connect < 0, ext_width, connect).reshape(-1)
    corners = jnp.take(extended, slot_index, axis=1, mode='fill', fill_value=0.0).reshape(combo_total, 3, 8, elem_total)
    gradient = jnp.zeros((combo_total, 3, 3, elem_total), extended.dtype)
    for corner in range(8):
        gradient = gradient + corners[:, :, None, corner, :] * gradients[corner][None, None, :, :]
    quadratic = lax.optimization_barrier(jnp.sum(gradient[:, :, :, None, :] * gradient[:, :, None, :, :], axis=1))
    green_strain = 0.5 * (gradient + jnp.swapaxes(gradient, 1, 2) + quadratic)
    strain_trace = green_strain[:, 0, 0] + green_strain[:, 1, 1] + green_strain[:, 2, 2]
    identity = jnp.eye(3, dtype=extended.dtype)[None, :, :, None]
    stress = lame[0] * strain_trace[:, None, None, :] * identity + 2.0 * lame[1] * green_strain
    piola = stress + lax.optimization_barrier(jnp.sum(gradient[:, :, :, None, :] * stress[:, None, :, :, :], axis=2))
    corner_forces = jnp.stack([lax.optimization_barrier(jnp.sum(piola * gradients[corner][None, None, :, :], axis=2)) for corner in range(8)], axis=2)
    return accum.at[:, slot_index].add(corner_forces.reshape(3 * combo_total, 8 * elem_total), mode='drop')

def from_partitions(packet_rows, slot_width):
    below_part = jnp.concatenate([jnp.zeros_like(packet_rows[:, :1, :, slot_width:]), packet_rows[:, :-1, :, slot_width:]], axis=1)
    above_part = jnp.concatenate([packet_rows[:, 1:, :, :slot_width], jnp.zeros_like(packet_rows[:, :1, :, :slot_width])], axis=1)
    return (below_part, above_part)

def from_sectors(packet_rows, slot_width):
    below_part = jnp.roll(packet_rows[..., slot_width:], 1, axis=0)
    above_part = jnp.roll(packet_rows[..., :slot_width], -1, axis=0)
    return (below_part, above_part)

def reference(amplitudes, mode_shapes, shape_grads, lame_params, connectivity, dom_sends, sector_sends):
    device_total = N_SECTOR * N_DOM
    table_rows = 3 * COMBOS
    flat_width = 3 * NODE_DEV
    shapes_dev = mode_shapes.reshape(MODES, 3, device_total, NODE_DEV).transpose(2, 0, 1, 3).reshape(device_total, MODES, flat_width)
    displaced = jnp.einsum('cm,vmx->vcx', amplitudes, shapes_dev, precision=lax.Precision.HIGHEST).reshape(device_total, table_rows, NODE_DEV)
    dom_lists = dom_sends.reshape(2, device_total, IF_DOM).transpose(1, 0, 2)
    sec_lists = sector_sends.reshape(2, device_total, IF_SEC).transpose(1, 0, 2)
    dom_packets = jax.vmap(take_slots)(displaced, dom_lists).reshape(N_SECTOR, N_DOM, table_rows, 2 * IF_DOM)
    sec_packets = jax.vmap(take_slots)(displaced, sec_lists).reshape(N_SECTOR, N_DOM, table_rows, 2 * IF_SEC)
    dom_below, dom_above = from_partitions(dom_packets, IF_DOM)
    sec_below, sec_above = from_sectors(sec_packets, IF_SEC)
    extended = jnp.concatenate([displaced.reshape(N_SECTOR, N_DOM, table_rows, NODE_DEV), dom_below, dom_above, sec_below, sec_above], axis=-1)
    extended = extended.reshape(device_total, table_rows, EXT_NODES)
    connect_dev = connectivity.reshape(8, device_total, ELEM_DEV).transpose(1, 0, 2)
    grads_dev = shape_grads.reshape(8, 3, device_total, ELEM_DEV).transpose(2, 0, 1, 3)
    lame_dev = lame_params.reshape(2, device_total, ELEM_DEV).transpose(1, 0, 2)

    def per_device(inputs_dev):
        table_dev, connect_one, grads_one, lame_one = inputs_dev
        start_table = jnp.zeros((table_rows, EXT_NODES), table_dev.dtype)
        return element_forces(start_table, table_dev, connect_one, grads_one, lame_one)
    slot_forces = lax.map(per_device, (extended, connect_dev, grads_dev, lame_dev))
    own_forces = slot_forces[..., :NODE_DEV]
    dom_back = slot_forces[..., NODE_DEV:NODE_DEV + 2 * IF_DOM].reshape(N_SECTOR, N_DOM, table_rows, 2 * IF_DOM)
    sec_back = slot_forces[..., NODE_DEV + 2 * IF_DOM:].reshape(N_SECTOR, N_DOM, table_rows, 2 * IF_SEC)
    back_below, back_above = from_partitions(dom_back, IF_DOM)
    returned_dom = jnp.concatenate([back_below, back_above], axis=-1).reshape(device_total, table_rows, 2 * IF_DOM)
    own_forces = jax.vmap(add_slots)(own_forces, dom_lists, returned_dom)
    back_below, back_above = from_sectors(sec_back, IF_SEC)
    returned_sec = jnp.concatenate([back_below, back_above], axis=-1).reshape(device_total, table_rows, 2 * IF_SEC)
    own_forces = jax.vmap(add_slots)(own_forces, sec_lists, returned_sec)
    nodal_out = own_forces.reshape(device_total, COMBOS, 3, NODE_DEV).transpose(1, 2, 0, 3).reshape(COMBOS, 3, NODES)
    modal_sum = jnp.einsum('vcx,vmx->cm', own_forces.reshape(device_total, COMBOS, flat_width), shapes_dev, precision=lax.Precision.HIGHEST)
    return (nodal_out, modal_sum / math.sqrt(3.0 * NODES))
```

```python
import functools
import math

import jax
import jax.numpy as jnp
from jax import lax
from jax.experimental import pallas as pl
from jax.experimental.pallas import tpu as pltpu
from jax.sharding import PartitionSpec as P

MESH = pl.DeviceIdType.MESH
F8 = jnp.float8_e4m3fn
BF = jnp.bfloat16
F32 = jnp.float32
TILE = 128
NT = (((1,), (1,)), ((), ()))


def bf_pieces(x):
    hi = x.astype(BF)
    return hi, (x - hi.astype(F32)).astype(BF)


def f8_pieces(x):
    a = x.astype(F8)
    rest = (x - a.astype(F32)) * 16.0
    b = rest.astype(F8)
    rest = (rest - b.astype(F32)) * 16.0
    return a, b, rest.astype(F8)


def joined(r, rows, unit):
    return r[:rows] * unit + (r[rows : 2 * rows] + r[2 * rows :] * 0.0625) * (unit * 0.0625)


def tile_hits(row, first, dtype_one, dtype_zero):
    near = row - first
    near = jnp.where((near >= 0) & (near < TILE), near, -1).astype(jnp.int8)
    slots = lax.broadcasted_iota(jnp.int32, (TILE, row.shape[1]), 0).astype(jnp.int8)
    return jnp.where(slots == near, dtype_one, dtype_zero)


def peak(x):
    return jnp.max(jnp.max(jnp.abs(x), axis=0, keepdims=True), axis=1, keepdims=True)


def stage_index(stage, y, x, c, z):
    return (x * 2 + c, y * 2 + z % 2, z // 2)[stage]


def stage_device(stage, i, y, x, c, z):
    if stage == 0:
        x, c = i // 2, i % 2
    elif stage == 1:
        y, z = i // 2, (z // 2) * 2 + i % 2
    else:
        z = i * 2 + z % 2
    return (y * 4 + (x % 2) * 2 + c, z * 2 + x // 2)


def kernel(
    scale, amp_ref, modes_ref, grads_ref, lame_ref, conn_ref, dsend_ref, ssend_ref,
    out_ref, modal_ref,
    hot, hot_send, hot_block, own_lhs, halo_lhs, corners, gmode, piola, forces,
    pk_dom, pk_sec, halo_dom, halo_sec, bk_dom, bk_sec, ret_dom, ret_sec, mine, theirs,
    fs_sem, fr_sem, bs_sem, br_sem, as_sem, ar_sem,
):
    n_sec, n_dom = lax.axis_size("sector"), lax.axis_size("dom")
    sec, dom = lax.axis_index("sector"), lax.axis_index("dom")
    modes, combos = amp_ref.shape
    nodes = modes_ref.shape[1]
    elems = conn_ref.shape[1]
    wd, ws = dsend_ref.shape[1], ssend_ref.shape[1]
    rows = 3 * modes
    frows = 3 * combos
    halo = 2 * wd + 2 * ws
    y, x, c, z = sec // 4, (dom % 2) * 2 + (sec // 2) % 2, sec % 2, dom // 2
    dom_lo, dom_hi = (sec, lax.rem(dom + n_dom - 1, n_dom)), (sec, lax.rem(dom + 1, n_dom))
    sec_lo, sec_hi = (lax.rem(sec + n_sec - 1, n_sec), dom), (lax.rem(sec + 1, n_sec), dom)
    halo_to = [dom_lo, dom_hi, sec_lo, sec_hi]
    me = [stage_index(s, y, x, c, z) for s in range(3)]
    groups = [
        [stage_device(s, lax.rem(me[s] + r, 8), y, x, c, z) for r in range(1, 8)] for s in range(3)
    ]

    barrier = pltpu.get_barrier_semaphore()
    everyone = halo_to + groups[0] + groups[1] + groups[2]
    for other in everyone:
        pl.semaphore_signal(barrier, inc=1, device_id=other, device_id_type=MESH)

    for first, width, send in ((0, wd, dsend_ref), (2 * wd, ws, ssend_ref)):
        for row in range(2):
            cols = pl.ds(first + row * width, width)
            slots = lax.broadcasted_iota(jnp.int32, (nodes, width), 0)
            hot_send[:, cols] = jnp.where(slots == send[row : row + 1, :], 1.0, 0.0).astype(BF)

    shapes = modes_ref[...]
    packets = jnp.dot(
        jnp.concatenate(bf_pieces(shapes), axis=0), hot_send[...], preferred_element_type=F32
    )
    packets = packets[:rows] + packets[rows:]
    for row in range(2):
        pk_dom[row] = packets[:, row * wd : (row + 1) * wd]
        pk_sec[row] = packets[:, 2 * wd + row * ws : 2 * wd + (row + 1) * ws]

    pl.semaphore_wait(barrier, len(everyone))
    forward = []
    for j, (src, dst) in enumerate(
        (
            (pk_dom.at[0], halo_dom.at[1]),
            (pk_dom.at[1], halo_dom.at[0]),
            (pk_sec.at[0], halo_sec.at[1]),
            (pk_sec.at[1], halo_sec.at[0]),
        )
    ):
        forward.append(
            pltpu.make_async_remote_copy(
                src_ref=src, dst_ref=dst, send_sem=fs_sem.at[j], recv_sem=fr_sem.at[j],
                device_id=halo_to[j], device_id_type=MESH,
            )
        )
        forward[-1].start()

    one8, zero8 = jnp.ones((TILE, elems), F8), jnp.zeros((TILE, elems), F8)

    def build(a, carry):
        row = conn_ref[pl.ds(a, 1), :]
        cols = pl.ds(pl.multiple_of(a * elems, elems), elems)
        for t in range((nodes + halo) // TILE):
            hot[pl.ds(t * TILE, TILE), cols] = tile_hits(row, t * TILE, one8, zero8)
        return carry

    lax.fori_loop(0, 8, build, 0)

    top = jnp.maximum(peak(shapes), 1e-30)
    for p, piece in enumerate(f8_pieces(shapes * (256.0 / top))):
        own_lhs[pl.ds(p * rows, rows), :] = piece
    own_unit = top * (1.0 / 256.0)

    def gather_own(a, carry):
        cols = pl.ds(pl.multiple_of(a * elems, elems), elems)
        r = jnp.dot(own_lhs[...], hot[0:nodes, cols], preferred_element_type=F32)
        corners[:, cols] = joined(r, rows, own_unit)
        return carry

    lax.fori_loop(0, 8, gather_own, 0)

    for copy in forward:
        copy.wait()
    has_lo = jnp.where(dom > 0, 1.0, 0.0).astype(F32)
    has_hi = jnp.where(dom < n_dom - 1, 1.0, 0.0).astype(F32)
    outside = jnp.concatenate(
        [halo_dom[0] * has_lo, halo_dom[1] * has_hi, halo_sec[0], halo_sec[1]], axis=1
    )
    top = jnp.maximum(peak(outside), 1e-30)
    for p, piece in enumerate(f8_pieces(outside * (256.0 / top))):
        halo_lhs[pl.ds(p * rows, rows), :] = piece
    halo_unit = top * (1.0 / 256.0)

    def gather_halo(a, carry):
        cols = pl.ds(pl.multiple_of(a * elems, elems), elems)
        r = jnp.dot(halo_lhs[...], hot[nodes : nodes + halo, cols], preferred_element_type=F32)
        corners[:, cols] = corners[:, cols] + joined(r, rows, halo_unit)
        return carry

    lax.fori_loop(0, 8, gather_halo, 0)

    def mode_gradient(e, carry):
        first = pl.multiple_of(e * 128, 128)
        lanes = pl.ds(first, 128)
        for m in range(modes // 16):
            acc = [None] * 9
            for a in range(8):
                for i in range(3):
                    u = corners[
                        pl.ds(i * modes + m * 16, 16),
                        pl.ds(pl.multiple_of(a * elems + first, 128), 128),
                    ]
                    for j in range(3):
                        term = u * grads_ref[j, pl.ds(a, 1), lanes]
                        acc[3 * i + j] = term if acc[3 * i + j] is None else acc[3 * i + j] + term
            for ij in range(9):
                hi, lo = bf_pieces(acc[ij])
                gmode[ij, pl.ds(m * 16, 16), lanes] = hi
                gmode[ij, pl.ds(modes + m * 16, 16), lanes] = hi
                gmode[ij, pl.ds(2 * modes + m * 16, 16), lanes] = lo
        return carry

    lax.fori_loop(0, elems // 128, mode_gradient, 0)

    amp_hi, amp_lo = bf_pieces(amp_ref[...].T)
    amp3 = jnp.concatenate([amp_hi, amp_lo, amp_hi], axis=1)

    def combine(ij, carry):
        piola[ij] = jnp.dot(amp3, gmode[ij], preferred_element_type=F32)
        return carry

    lax.fori_loop(0, 9, combine, 0)

    def stress_rows(r, carry):
        part = pl.ds(pl.multiple_of(r * 8, 8), 8)

        def stress_cols(e, keep):
            lanes = pl.ds(pl.multiple_of(e * 128, 128), 128)
            g = [[piola[3 * i + j, part, lanes] for j in range(3)] for i in range(3)]
            lam, mu = lame_ref[0:1, lanes], lame_ref[1:2, lanes]
            twice = [[None] * 3 for _ in range(3)]
            for i in range(3):
                for j in range(i, 3):
                    quad = g[0][i] * g[0][j] + g[1][i] * g[1][j] + g[2][i] * g[2][j]
                    twice[i][j] = twice[j][i] = g[i][j] + g[j][i] + quad
            trace = (twice[0][0] + twice[1][1] + twice[2][2]) * (0.5 * lam)
            s = [[None] * 3 for _ in range(3)]
            for i in range(3):
                for j in range(i, 3):
                    v = mu * twice[i][j]
                    s[i][j] = s[j][i] = v + trace if i == j else v
            for i in range(3):
                for j in range(3):
                    p = s[i][j] + g[i][0] * s[0][j] + g[i][1] * s[1][j] + g[i][2] * s[2][j]
                    piola[3 * i + j, part, lanes] = p
            return keep

        return lax.fori_loop(0, elems // 128, stress_cols, carry)

    lax.fori_loop(0, combos // 8, stress_rows, 0)

    def project(ij, acc):
        both = jnp.concatenate(bf_pieces(piola[ij]), axis=0)
        return acc + lax.dot_general(
            gmode[ij, pl.ds(modes, 2 * modes), :], both, NT, preferred_element_type=F32
        )

    acc = lax.fori_loop(0, 9, project, jnp.zeros((2 * modes, 2 * combos), F32))
    acc = acc[:modes] + acc[modes:]
    acc = acc[:, :combos] + acc[:, combos:]
    half = modes // 2
    mine[0] = jnp.concatenate([acc[:half], acc[half:]], axis=1)

    def send_stage(s):
        copies = []
        for r, other in enumerate(groups[s]):
            copies.append(
                pltpu.make_async_remote_copy(
                    src_ref=mine.at[s], dst_ref=theirs.at[s, me[s]],
                    send_sem=as_sem.at[s, r], recv_sem=ar_sem.at[s, r],
                    device_id=other, device_id_type=MESH,
                )
            )
            copies[-1].start()
        return copies

    def end_stage(s, copies):
        theirs[s, me[s]] = mine[s]
        for copy in copies:
            copy.wait()
        total = theirs[s, 0]
        for q in range(1, 8):
            total = total + theirs[s, q]
        return total

    stage0 = send_stage(0)

    def corner_forces(e, carry):
        first = pl.multiple_of(e * 128, 128)
        lanes = pl.ds(first, 128)
        for q in range(combos // 32):
            part = pl.ds(q * 32, 32)
            for i in range(3):
                p = [piola[3 * i + j, part, lanes] for j in range(3)]
                for a in range(8):
                    f = (
                        p[0] * grads_ref[0, pl.ds(a, 1), lanes]
                        + p[1] * grads_ref[1, pl.ds(a, 1), lanes]
                        + p[2] * grads_ref[2, pl.ds(a, 1), lanes]
                    )
                    cols = pl.ds(pl.multiple_of(a * elems + first, 128), 128)
                    for t, piece in enumerate(bf_pieces(f)):
                        forces[pl.ds(t * frows + i * combos + q * 32, 32), cols] = piece
        return carry

    lax.fori_loop(0, elems // 128, corner_forces, 0)

    def scatter(first, width):
        def fill(a, carry):
            near = (conn_ref[pl.ds(a, 1), :] - first).astype(jnp.int16)
            slots = lax.broadcasted_iota(jnp.int16, (width, elems), 0)
            cols = pl.ds(pl.multiple_of(a * elems, elems), elems)
            hot_block[0:width, cols] = jnp.where(slots == near, jnp.ones((), BF), jnp.zeros((), BF))
            return carry

        lax.fori_loop(0, 8, fill, 0)
        r = lax.dot_general(forces[...], hot_block[0:width, :], NT, preferred_element_type=F32)
        return r[:frows] + r[frows:]

    backward = []

    def send_back(j, src, dst):
        backward.append(
            pltpu.make_async_remote_copy(
                src_ref=src, dst_ref=dst, send_sem=bs_sem.at[j], recv_sem=br_sem.at[j],
                device_id=halo_to[j], device_id_type=MESH,
            )
        )
        backward[-1].start()

    bk_dom[0] = scatter(nodes, wd)
    send_back(0, bk_dom.at[0], ret_dom.at[1])
    bk_dom[1] = scatter(nodes + wd, wd)
    send_back(1, bk_dom.at[1], ret_dom.at[0])
    both = scatter(nodes + 2 * wd, 2 * ws)
    bk_sec[0] = both[:, :ws]
    bk_sec[1] = both[:, ws:]
    send_back(2, bk_sec.at[0], ret_sec.at[1])
    send_back(3, bk_sec.at[1], ret_sec.at[0])

    mine[1] = end_stage(0, stage0)
    stage1 = send_stage(1)

    def own_block(b, carry):
        first = pl.multiple_of(b * 256, 256)
        out_ref[:, pl.ds(first, 256)] = scatter(first, 256)
        return carry

    blocks = nodes // 256
    lax.fori_loop(0, blocks // 2, own_block, 0)
    mine[2] = end_stage(1, stage1)
    stage2 = send_stage(2)
    lax.fori_loop(blocks // 2, blocks, own_block, 0)
    total = end_stage(2, stage2) * scale
    modal_ref[0:half, :] = total[:, :combos]
    modal_ref[half:modes, :] = total[:, combos:]

    for copy in backward:
        copy.wait()
    returned = jnp.concatenate(
        [ret_dom[0] * has_lo, ret_dom[1] * has_hi, ret_sec[0], ret_sec[1]], axis=1
    )
    r = lax.dot_general(
        jnp.concatenate(bf_pieces(returned), axis=0), hot_send[...], NT, preferred_element_type=F32
    )
    out_ref[...] = out_ref[...] + (r[:frows] + r[frows:])


def local(amplitudes, mode_shapes, shape_grads, lame_params, connectivity, dom_sends, sector_sends):
    modes, _, nodes = mode_shapes.shape
    combos = amplitudes.shape[0]
    elems = connectivity.shape[1]
    wd, ws = dom_sends.shape[1], sector_sends.shape[1]
    rows, frows, halo = 3 * modes, 3 * combos, 2 * wd + 2 * ws
    all_nodes = nodes * lax.axis_size("sector") * lax.axis_size("dom")
    vmem = pl.BlockSpec(memory_space=pltpu.VMEM)
    dma = pltpu.SemaphoreType.DMA
    nodal, modal = pl.pallas_call(
        functools.partial(kernel, 1.0 / math.sqrt(3.0 * all_nodes)),
        out_shape=(
            jax.ShapeDtypeStruct((frows, nodes), F32),
            jax.ShapeDtypeStruct((modes, combos), F32),
        ),
        in_specs=[vmem] * 7,
        out_specs=(vmem, vmem),
        scratch_shapes=[
            pltpu.VMEM((nodes + halo, 8 * elems), F8),
            pltpu.VMEM((nodes, halo), BF),
            pltpu.VMEM((256, 8 * elems), BF),
            pltpu.VMEM((3 * rows, nodes), F8),
            pltpu.VMEM((3 * rows, halo), F8),
            pltpu.VMEM((rows, 8 * elems), F32),
            pltpu.VMEM((9, 3 * modes, elems), BF),
            pltpu.VMEM((9, combos, elems), F32),
            pltpu.VMEM((2 * frows, 8 * elems), BF),
            pltpu.VMEM((2, rows, wd), F32),
            pltpu.VMEM((2, rows, ws), F32),
            pltpu.VMEM((2, rows, wd), F32),
            pltpu.VMEM((2, rows, ws), F32),
            pltpu.VMEM((2, frows, wd), F32),
            pltpu.VMEM((2, frows, ws), F32),
            pltpu.VMEM((2, frows, wd), F32),
            pltpu.VMEM((2, frows, ws), F32),
            pltpu.VMEM((3, modes // 2, 2 * combos), F32),
            pltpu.VMEM((3, 8, modes // 2, 2 * combos), F32),
            dma((4,)), dma((4,)), dma((4,)), dma((4,)), dma((3, 7)), dma((3, 7)),
        ],
        compiler_params=pltpu.CompilerParams(
            collective_id=0, has_side_effects=True, vmem_limit_bytes=56 << 20
        ),
    )(
        amplitudes.T,
        mode_shapes.transpose(1, 0, 2).reshape(rows, nodes),
        shape_grads.transpose(1, 0, 2),
        lame_params,
        connectivity,
        dom_sends,
        sector_sends,
    )
    return nodal.reshape(3, combos, nodes).transpose(1, 0, 2), modal.T


def solution(mesh):
    placed = (
        P(),
        P(None, None, ("sector", "dom")),
        P(None, None, ("sector", "dom")),
        P(None, ("sector", "dom")),
        P(None, ("sector", "dom")),
        P(None, ("sector", "dom")),
        P(None, ("sector", "dom")),
    )
    return jax.shard_map(
        local,
        mesh=mesh,
        in_specs=placed,
        out_specs=(P(None, None, ("sector", "dom")), P()),
        check_vma=False,
    )
```

```python
import functools
import math

import jax
import jax.numpy as jnp
from jax import lax
from jax.experimental import pallas as pl
from jax.experimental.pallas import tpu as pltpu
from jax.sharding import PartitionSpec as P

MESH = pl.DeviceIdType.MESH
F8 = jnp.float8_e4m3fn
BF = jnp.bfloat16
F32 = jnp.float32
TILE = 128
NT = (((1,), (1,)), ((), ()))


def bf_pieces(x):
    hi = x.astype(BF)
    return hi, (x - hi.astype(F32)).astype(BF)


def f8_pieces(x):
    a = x.astype(F8)
    rest = (x - a.astype(F32)) * 16.0
    b = rest.astype(F8)
    rest = (rest - b.astype(F32)) * 16.0
    return a, b, rest.astype(F8)


def joined(r, rows, unit):
    return r[:rows] * unit + (r[rows : 2 * rows] + r[2 * rows :] * 0.0625) * (unit * 0.0625)


def tile_hits(row, first, dtype_one, dtype_zero):
    near = row - first
    near = jnp.where((near >= 0) & (near < TILE), near, -1).astype(jnp.int8)
    slots = lax.broadcasted_iota(jnp.int32, (TILE, row.shape[1]), 0).astype(jnp.int8)
    return jnp.where(slots == near, dtype_one, dtype_zero)


def peak(x):
    return jnp.max(jnp.max(jnp.abs(x), axis=0, keepdims=True), axis=1, keepdims=True)


def stage_index(stage, y, x, c, z):
    return (z // 2, y * 2 + z % 2, x * 2 + c)[stage]


def stage_device(stage, i, y, x, c, z):
    if stage == 0:
        z = i * 2 + z % 2
    elif stage == 1:
        y, z = i // 2, (z // 2) * 2 + i % 2
    else:
        x, c = i // 2, i % 2
    return (y * 4 + (x % 2) * 2 + c, z * 2 + x // 2)


def kernel(
    scale, amp_hbm, modes_hbm, grads_hbm, lame_hbm, conn_hbm, dsend_hbm, ssend_hbm,
    out_ref, modal_ref,
    amp_ref, modes_ref, grads_ref, lame_ref, conn_ref, dsend_ref, ssend_ref,
    hot, hot_send, hot_block, own_lhs, halo_lhs, corners, gmode, piola, forces,
    pk_dom, pk_sec, halo_dom, halo_sec, bk_dom, bk_sec, ret_dom, ret_sec, mine, theirs,
    in_sem, fs_sem, fr_sem, bs_sem, br_sem, as_sem, ar_sem,
):
    n_sec, n_dom = lax.axis_size("sector"), lax.axis_size("dom")
    sec, dom = lax.axis_index("sector"), lax.axis_index("dom")
    modes, combos = amp_ref.shape
    nodes = modes_ref.shape[1]
    elems = conn_ref.shape[1]
    wd, ws = dsend_ref.shape[1], ssend_ref.shape[1]
    rows = 3 * modes
    frows = 3 * combos
    halo = 2 * wd + 2 * ws
    y, x, c, z = sec // 4, (dom % 2) * 2 + (sec // 2) % 2, sec % 2, dom // 2
    dom_lo, dom_hi = (sec, lax.rem(dom + n_dom - 1, n_dom)), (sec, lax.rem(dom + 1, n_dom))
    sec_lo, sec_hi = (lax.rem(sec + n_sec - 1, n_sec), dom), (lax.rem(sec + 1, n_sec), dom)
    halo_to = [dom_lo, dom_hi, sec_lo, sec_hi]
    me = [stage_index(s, y, x, c, z) for s in range(3)]
    groups = [
        [stage_device(s, lax.rem(me[s] + r, 8), y, x, c, z) for r in range(1, 8)] for s in range(3)
    ]

    loads = [
        pltpu.make_async_copy(src, dst, in_sem.at[j])
        for j, (src, dst) in enumerate(
            (
                (dsend_hbm, dsend_ref),
                (ssend_hbm, ssend_ref),
                (modes_hbm, modes_ref),
                (conn_hbm, conn_ref),
                (grads_hbm, grads_ref),
                (amp_hbm, amp_ref),
                (lame_hbm, lame_ref),
            )
        )
    ]
    for load in loads:
        load.start()
    barrier = pltpu.get_barrier_semaphore()
    everyone = halo_to + groups[0] + groups[1] + groups[2]
    for other in everyone:
        pl.semaphore_signal(barrier, inc=1, device_id=other, device_id_type=MESH)

    loads[0].wait()
    loads[1].wait()
    for first, width, send in ((0, wd, dsend_ref), (2 * wd, ws, ssend_ref)):
        for row in range(2):
            cols = pl.ds(first + row * width, width)
            slots = lax.broadcasted_iota(jnp.int32, (nodes, width), 0)
            hot_send[:, cols] = jnp.where(slots == send[row : row + 1, :], 1.0, 0.0).astype(BF)

    loads[2].wait()
    shapes = modes_ref[...]
    packets = jnp.dot(
        jnp.concatenate(bf_pieces(shapes), axis=0), hot_send[...], preferred_element_type=F32
    )
    packets = packets[:rows] + packets[rows:]
    for row in range(2):
        pk_dom[row] = packets[:, row * wd : (row + 1) * wd]
        pk_sec[row] = packets[:, 2 * wd + row * ws : 2 * wd + (row + 1) * ws]

    pl.semaphore_wait(barrier, len(everyone))
    forward = []
    for j, (src, dst) in enumerate(
        (
            (pk_dom.at[0], halo_dom.at[1]),
            (pk_dom.at[1], halo_dom.at[0]),
            (pk_sec.at[0], halo_sec.at[1]),
            (pk_sec.at[1], halo_sec.at[0]),
        )
    ):
        forward.append(
            pltpu.make_async_remote_copy(
                src_ref=src, dst_ref=dst, send_sem=fs_sem.at[j], recv_sem=fr_sem.at[j],
                device_id=halo_to[j], device_id_type=MESH,
            )
        )
        forward[-1].start()

    for load in loads[3:]:
        load.wait()
    one8, zero8 = jnp.ones((TILE, elems), F8), jnp.zeros((TILE, elems), F8)

    def gather(lhs, first, count, a, unit):
        room = hot.at[a % 2]
        for t in range(count // TILE):
            room[pl.ds(t * TILE, TILE), :] = tile_hits(
                conn_ref[pl.ds(a, 1), :], first + t * TILE, one8, zero8
            )
        r = jnp.dot(lhs[...], room[0:count, :], preferred_element_type=F32)
        return joined(r, rows, unit)

    top = jnp.maximum(peak(shapes), 1e-30)
    for p, piece in enumerate(f8_pieces(shapes * (256.0 / top))):
        own_lhs[pl.ds(p * rows, rows), :] = piece
    own_unit = top * (1.0 / 256.0)

    for a in range(8):
        corners[:, pl.ds(a * elems, elems)] = gather(own_lhs, 0, nodes, a, own_unit)

    for copy in forward:
        copy.wait()
    has_lo = jnp.where(dom > 0, 1.0, 0.0).astype(F32)
    has_hi = jnp.where(dom < n_dom - 1, 1.0, 0.0).astype(F32)
    outside = jnp.concatenate(
        [halo_dom[0] * has_lo, halo_dom[1] * has_hi, halo_sec[0], halo_sec[1]], axis=1
    )
    top = jnp.maximum(peak(outside), 1e-30)
    for p, piece in enumerate(f8_pieces(outside * (256.0 / top))):
        halo_lhs[pl.ds(p * rows, rows), :] = piece
    halo_unit = top * (1.0 / 256.0)

    for a in range(8):
        cols = pl.ds(a * elems, elems)
        corners[:, cols] = corners[:, cols] + gather(halo_lhs, nodes, halo, a, halo_unit)

    def mode_gradient(e, carry):
        first = pl.multiple_of(e * 128, 128)
        lanes = pl.ds(first, 128)
        for m in range(modes // 16):
            acc = [None] * 9
            for a in range(8):
                for i in range(3):
                    u = corners[
                        pl.ds(i * modes + m * 16, 16),
                        pl.ds(pl.multiple_of(a * elems + first, 128), 128),
                    ]
                    for j in range(3):
                        term = u * grads_ref[j, pl.ds(a, 1), lanes]
                        acc[3 * i + j] = term if acc[3 * i + j] is None else acc[3 * i + j] + term
            for ij in range(9):
                hi, lo = bf_pieces(acc[ij])
                cols = pl.ds(pl.multiple_of(ij * elems + first, 128), 128)
                gmode[pl.ds(m * 16, 16), cols] = hi
                gmode[pl.ds(modes + m * 16, 16), cols] = hi
                gmode[pl.ds(2 * modes + m * 16, 16), cols] = lo
        return carry

    lax.fori_loop(0, elems // 128, mode_gradient, 0)

    amp_hi, amp_lo = bf_pieces(amp_ref[...].T)
    amp3 = jnp.concatenate([amp_hi, amp_lo, amp_hi], axis=1)

    piola[...] = jnp.dot(amp3, gmode[...], preferred_element_type=F32)

    def stress_rows(r, carry):
        part = pl.ds(pl.multiple_of(r * 8, 8), 8)

        def stress_cols(e, keep):
            first = pl.multiple_of(e * 128, 128)
            lanes = pl.ds(first, 128)
            at = [pl.ds(pl.multiple_of(ij * elems + first, 128), 128) for ij in range(9)]
            g = [[piola[part, at[3 * i + j]] for j in range(3)] for i in range(3)]
            lam, mu = lame_ref[0:1, lanes], lame_ref[1:2, lanes]
            twice = [[None] * 3 for _ in range(3)]
            for i in range(3):
                for j in range(i, 3):
                    quad = g[0][i] * g[0][j] + g[1][i] * g[1][j] + g[2][i] * g[2][j]
                    twice[i][j] = twice[j][i] = g[i][j] + g[j][i] + quad
            trace = (twice[0][0] + twice[1][1] + twice[2][2]) * (0.5 * lam)
            s = [[None] * 3 for _ in range(3)]
            for i in range(3):
                for j in range(i, 3):
                    v = mu * twice[i][j]
                    s[i][j] = s[j][i] = v + trace if i == j else v
            for i in range(3):
                for j in range(3):
                    p = s[i][j] + g[i][0] * s[0][j] + g[i][1] * s[1][j] + g[i][2] * s[2][j]
                    piola[part, at[3 * i + j]] = p
            return keep

        return lax.fori_loop(0, elems // 128, stress_cols, carry)

    lax.fori_loop(0, combos // 8, stress_rows, 0)

    both = jnp.concatenate(bf_pieces(piola[...]), axis=0)
    acc = lax.dot_general(
        gmode[modes : 3 * modes, :], both, NT, preferred_element_type=F32
    )
    acc = acc[:modes] + acc[modes:]
    acc = acc[:, :combos] + acc[:, combos:]
    half = modes // 2
    mine[0] = jnp.concatenate([acc[:half], acc[half:]], axis=1)

    def send_stage(s):
        copies = []
        for r, other in enumerate(groups[s]):
            copies.append(
                pltpu.make_async_remote_copy(
                    src_ref=mine.at[s], dst_ref=theirs.at[s, me[s]],
                    send_sem=as_sem.at[s, r], recv_sem=ar_sem.at[s, r],
                    device_id=other, device_id_type=MESH,
                )
            )
            copies[-1].start()
        return copies

    def end_stage(s, copies):
        theirs[s, me[s]] = mine[s]
        for copy in copies:
            copy.wait()
        total = theirs[s, 0]
        for q in range(1, 8):
            total = total + theirs[s, q]
        return total

    stage0 = send_stage(0)

    def corner_forces(e, carry):
        first = pl.multiple_of(e * 128, 128)
        lanes = pl.ds(first, 128)
        for q in range(combos // 32):
            part = pl.ds(q * 32, 32)
            for i in range(3):
                p = [
                    piola[part, pl.ds(pl.multiple_of((3 * i + j) * elems + first, 128), 128)]
                    for j in range(3)
                ]
                for a in range(8):
                    f = (
                        p[0] * grads_ref[0, pl.ds(a, 1), lanes]
                        + p[1] * grads_ref[1, pl.ds(a, 1), lanes]
                        + p[2] * grads_ref[2, pl.ds(a, 1), lanes]
                    )
                    cols = pl.ds(pl.multiple_of(a * elems + first, 128), 128)
                    for t, piece in enumerate(bf_pieces(f)):
                        forces[pl.ds(t * frows + i * combos + q * 32, 32), cols] = piece
        return carry

    lax.fori_loop(0, elems // 128, corner_forces, 0)

    def scatter(first, width):
        for a in range(8):
            near = (conn_ref[a : a + 1, :] - first).astype(jnp.int16)
            slots = lax.broadcasted_iota(jnp.int16, (width, elems), 0)
            cols = pl.ds(a * elems, elems)
            hot_block[0:width, cols] = jnp.where(slots == near, jnp.ones((), BF), jnp.zeros((), BF))
        r = lax.dot_general(forces[...], hot_block[0:width, :], NT, preferred_element_type=F32)
        return r[:frows] + r[frows:]

    backward = []

    def send_back(j, src, dst):
        backward.append(
            pltpu.make_async_remote_copy(
                src_ref=src, dst_ref=dst, send_sem=bs_sem.at[j], recv_sem=br_sem.at[j],
                device_id=halo_to[j], device_id_type=MESH,
            )
        )
        backward[-1].start()

    bk_dom[0] = scatter(nodes, wd)
    mine[1] = end_stage(0, stage0)
    stage1 = send_stage(1)
    bk_dom[1] = scatter(nodes + wd, wd)
    both = scatter(nodes + 2 * wd, 2 * ws)
    bk_sec[0] = both[:, :ws]
    bk_sec[1] = both[:, ws:]
    mine[2] = end_stage(1, stage1)
    stage2 = send_stage(2)
    send_back(0, bk_dom.at[0], ret_dom.at[1])
    send_back(1, bk_dom.at[1], ret_dom.at[0])
    send_back(2, bk_sec.at[0], ret_sec.at[1])
    send_back(3, bk_sec.at[1], ret_sec.at[0])

    def own_block(b, carry):
        first = pl.multiple_of(b * 256, 256)
        out_ref[:, pl.ds(first, 256)] = scatter(first, 256)
        return carry

    blocks = nodes // 256
    lax.fori_loop(0, blocks, own_block, 0)
    total = end_stage(2, stage2) * scale
    modal_ref[0:half, :] = total[:, :combos]
    modal_ref[half:modes, :] = total[:, combos:]

    for copy in backward:
        copy.wait()
    returned = jnp.concatenate(
        [ret_dom[0] * has_lo, ret_dom[1] * has_hi, ret_sec[0], ret_sec[1]], axis=1
    )
    r = lax.dot_general(
        jnp.concatenate(bf_pieces(returned), axis=0), hot_send[...], NT, preferred_element_type=F32
    )
    out_ref[...] = out_ref[...] + (r[:frows] + r[frows:])


def local(amplitudes, mode_shapes, shape_grads, lame_params, connectivity, dom_sends, sector_sends):
    modes, _, nodes = mode_shapes.shape
    combos = amplitudes.shape[0]
    elems = connectivity.shape[1]
    wd, ws = dom_sends.shape[1], sector_sends.shape[1]
    rows, frows, halo = 3 * modes, 3 * combos, 2 * wd + 2 * ws
    all_nodes = nodes * lax.axis_size("sector") * lax.axis_size("dom")
    vmem = pl.BlockSpec(memory_space=pltpu.VMEM)
    dma = pltpu.SemaphoreType.DMA
    nodal, modal = pl.pallas_call(
        functools.partial(kernel, 1.0 / math.sqrt(3.0 * all_nodes)),
        out_shape=(
            jax.ShapeDtypeStruct((frows, nodes), F32),
            jax.ShapeDtypeStruct((modes, combos), F32),
        ),
        in_specs=[pl.BlockSpec(memory_space=pltpu.HBM)] * 7,
        out_specs=(vmem, vmem),
        scratch_shapes=[
            pltpu.VMEM((modes, combos), F32),
            pltpu.VMEM((rows, nodes), F32),
            pltpu.VMEM((3, 8, elems), F32),
            pltpu.VMEM((2, elems), F32),
            pltpu.VMEM((8, elems), jnp.int32),
            pltpu.VMEM((2, wd), jnp.int32),
            pltpu.VMEM((2, ws), jnp.int32),
            pltpu.VMEM((2, nodes, elems), F8),
            pltpu.VMEM((nodes, halo), BF),
            pltpu.VMEM((256, 8 * elems), BF),
            pltpu.VMEM((3 * rows, nodes), F8),
            pltpu.VMEM((3 * rows, halo), F8),
            pltpu.VMEM((rows, 8 * elems), F32),
            pltpu.VMEM((3 * modes, 9 * elems), BF),
            pltpu.VMEM((combos, 9 * elems), F32),
            pltpu.VMEM((2 * frows, 8 * elems), BF),
            pltpu.VMEM((2, rows, wd), F32),
            pltpu.VMEM((2, rows, ws), F32),
            pltpu.VMEM((2, rows, wd), F32),
            pltpu.VMEM((2, rows, ws), F32),
            pltpu.VMEM((2, frows, wd), F32),
            pltpu.VMEM((2, frows, ws), F32),
            pltpu.VMEM((2, frows, wd), F32),
            pltpu.VMEM((2, frows, ws), F32),
            pltpu.VMEM((3, modes // 2, 2 * combos), F32),
            pltpu.VMEM((3, 8, modes // 2, 2 * combos), F32),
            dma((7,)), dma((4,)), dma((4,)), dma((4,)), dma((4,)), dma((3, 7)), dma((3, 7)),
        ],
        compiler_params=pltpu.CompilerParams(
            collective_id=0, has_side_effects=True, vmem_limit_bytes=56 << 20
        ),
    )(
        amplitudes.T,
        mode_shapes.transpose(1, 0, 2).reshape(rows, nodes),
        shape_grads.transpose(1, 0, 2),
        lame_params,
        connectivity,
        dom_sends,
        sector_sends,
    )
    return nodal.reshape(3, combos, nodes).transpose(1, 0, 2), modal.T


def solution(mesh):
    placed = (
        P(),
        P(None, None, ("sector", "dom")),
        P(None, None, ("sector", "dom")),
        P(None, ("sector", "dom")),
        P(None, ("sector", "dom")),
        P(None, ("sector", "dom")),
        P(None, ("sector", "dom")),
    )
    return jax.shard_map(
        local,
        mesh=mesh,
        in_specs=placed,
        out_specs=(P(None, None, ("sector", "dom")), P()),
        check_vma=False,
    )
```

```python
import functools
import math

import jax
import jax.numpy as jnp
from jax import lax
from jax.experimental import pallas as pl
from jax.experimental.pallas import tpu as pltpu
from jax.sharding import PartitionSpec as P

MESH = pl.DeviceIdType.MESH
F8 = jnp.float8_e4m3fn
BF = jnp.bfloat16
F32 = jnp.float32
TILE = 128
NT = (((1,), (1,)), ((), ()))


def bf_pieces(x):
    hi = x.astype(BF)
    return hi, (x - hi.astype(F32)).astype(BF)


def f8_pieces(x):
    a = x.astype(F8)
    rest = (x - a.astype(F32)) * 16.0
    b = rest.astype(F8)
    rest = (rest - b.astype(F32)) * 16.0
    return a, b, rest.astype(F8)


def joined(r, rows, unit):
    return r[:rows] * unit + (r[rows : 2 * rows] + r[2 * rows :] * 0.0625) * (unit * 0.0625)


def tile_hits(row, first, dtype_one, dtype_zero):
    near = row - first
    near = jnp.where((near >= 0) & (near < TILE), near, -1).astype(jnp.int8)
    slots = lax.broadcasted_iota(jnp.int32, (TILE, row.shape[1]), 0).astype(jnp.int8)
    return jnp.where(slots == near, dtype_one, dtype_zero)


def peak(x):
    return jnp.max(jnp.max(jnp.abs(x), axis=0, keepdims=True), axis=1, keepdims=True)


def stage_index(stage, y, x, c, z):
    return (z // 2, y * 2 + z % 2, x * 2 + c)[stage]


def stage_device(stage, i, y, x, c, z):
    if stage == 0:
        z = i * 2 + z % 2
    elif stage == 1:
        y, z = i // 2, (z // 2) * 2 + i % 2
    else:
        x, c = i // 2, i % 2
    return (y * 4 + (x % 2) * 2 + c, z * 2 + x // 2)


def kernel(
    scale, amp_hbm, modes_hbm, grads_hbm, lame_hbm, conn_hbm, dsend_hbm, ssend_hbm,
    out_ref, modal_ref,
    amp_ref, modes_ref, grads_ref, lame_ref, conn_ref, dsend_ref, ssend_ref,
    hot, hot_send, hot_block, own_lhs, halo_lhs, corners, gmode, piola, forces,
    pk_dom, pk_sec, halo_dom, halo_sec, bk_dom, bk_sec, ret_dom, ret_sec, mine, theirs,
    in_sem, fs_sem, fr_sem, bs_sem, br_sem, as_sem, ar_sem,
):
    n_sec, n_dom = lax.axis_size("sector"), lax.axis_size("dom")
    sec, dom = lax.axis_index("sector"), lax.axis_index("dom")
    modes, combos = amp_ref.shape
    nodes = modes_ref.shape[1]
    elems = conn_ref.shape[1]
    wd, ws = dsend_ref.shape[1], ssend_ref.shape[1]
    rows = 3 * modes
    frows = 3 * combos
    halo = 2 * wd + 2 * ws
    y, x, c, z = sec // 4, (dom % 2) * 2 + (sec // 2) % 2, sec % 2, dom // 2
    dom_lo, dom_hi = (sec, lax.rem(dom + n_dom - 1, n_dom)), (sec, lax.rem(dom + 1, n_dom))
    sec_lo, sec_hi = (lax.rem(sec + n_sec - 1, n_sec), dom), (lax.rem(sec + 1, n_sec), dom)
    halo_to = [dom_lo, dom_hi, sec_lo, sec_hi]
    me = [stage_index(s, y, x, c, z) for s in range(3)]
    groups = [
        [stage_device(s, lax.rem(me[s] + r, 8), y, x, c, z) for r in range(1, 8)] for s in range(3)
    ]

    loads = [
        pltpu.make_async_copy(src, dst, in_sem.at[j])
        for j, (src, dst) in enumerate(
            (
                (dsend_hbm, dsend_ref),
                (ssend_hbm, ssend_ref),
                (modes_hbm, modes_ref),
                (conn_hbm, conn_ref),
                (grads_hbm, grads_ref),
                (amp_hbm, amp_ref),
                (lame_hbm, lame_ref),
            )
        )
    ]
    for load in loads:
        load.start()
    barrier = pltpu.get_barrier_semaphore()
    everyone = halo_to + groups[0] + groups[1] + groups[2]
    for other in everyone:
        pl.semaphore_signal(barrier, inc=1, device_id=other, device_id_type=MESH)

    loads[0].wait()
    loads[1].wait()
    for first, width, send in ((0, wd, dsend_ref), (2 * wd, ws, ssend_ref)):
        for row in range(2):
            cols = pl.ds(first + row * width, width)
            slots = lax.broadcasted_iota(jnp.int32, (nodes, width), 0)
            hot_send[:, cols] = jnp.where(slots == send[row : row + 1, :], 1.0, 0.0).astype(BF)

    loads[2].wait()
    shapes = modes_ref[...]
    packets = jnp.dot(
        jnp.concatenate(bf_pieces(shapes), axis=0), hot_send[...], preferred_element_type=F32
    )
    packets = packets[:rows] + packets[rows:]
    for row in range(2):
        pk_dom[row] = packets[:, row * wd : (row + 1) * wd]
        pk_sec[row] = packets[:, 2 * wd + row * ws : 2 * wd + (row + 1) * ws]

    pl.semaphore_wait(barrier, len(everyone))
    forward = []
    for j, (src, dst) in enumerate(
        (
            (pk_dom.at[0], halo_dom.at[1]),
            (pk_dom.at[1], halo_dom.at[0]),
            (pk_sec.at[0], halo_sec.at[1]),
            (pk_sec.at[1], halo_sec.at[0]),
        )
    ):
        forward.append(
            pltpu.make_async_remote_copy(
                src_ref=src, dst_ref=dst, send_sem=fs_sem.at[j], recv_sem=fr_sem.at[j],
                device_id=halo_to[j], device_id_type=MESH,
            )
        )
        forward[-1].start()

    for load in loads[3:]:
        load.wait()
    one8, zero8 = jnp.ones((TILE, elems), F8), jnp.zeros((TILE, elems), F8)

    def gather(lhs, first, count, a, unit):
        room = hot.at[a % 2]
        for t in range(count // TILE):
            room[pl.ds(t * TILE, TILE), :] = tile_hits(
                conn_ref[pl.ds(a, 1), :], first + t * TILE, one8, zero8
            )
        r = jnp.dot(lhs[...], room[0:count, :], preferred_element_type=F32)
        return joined(r, rows, unit)

    top = jnp.maximum(peak(shapes), 1e-30)
    for p, piece in enumerate(f8_pieces(shapes * (256.0 / top))):
        own_lhs[pl.ds(p * rows, rows), :] = piece
    own_unit = top * (1.0 / 256.0)

    for a in range(8):
        corners[:, pl.ds(a * elems, elems)] = gather(own_lhs, 0, nodes, a, own_unit)

    for copy in forward:
        copy.wait()
    has_lo = jnp.where(dom > 0, 1.0, 0.0).astype(F32)
    has_hi = jnp.where(dom < n_dom - 1, 1.0, 0.0).astype(F32)
    outside = jnp.concatenate(
        [halo_dom[0] * has_lo, halo_dom[1] * has_hi, halo_sec[0], halo_sec[1]], axis=1
    )
    top = jnp.maximum(peak(outside), 1e-30)
    for p, piece in enumerate(f8_pieces(outside * (256.0 / top))):
        halo_lhs[pl.ds(p * rows, rows), :] = piece
    halo_unit = top * (1.0 / 256.0)

    for a in range(8):
        cols = pl.ds(a * elems, elems)
        corners[:, cols] = corners[:, cols] + gather(halo_lhs, nodes, halo, a, halo_unit)

    def mode_gradient(e, carry):
        first = pl.multiple_of(e * 128, 128)
        lanes = pl.ds(first, 128)
        for m in range(modes // 16):
            acc = [None] * 9
            for a in range(8):
                for i in range(3):
                    u = corners[
                        pl.ds(i * modes + m * 16, 16),
                        pl.ds(pl.multiple_of(a * elems + first, 128), 128),
                    ]
                    for j in range(3):
                        term = u * grads_ref[j, pl.ds(a, 1), lanes]
                        acc[3 * i + j] = term if acc[3 * i + j] is None else acc[3 * i + j] + term
            for ij in range(9):
                hi, lo = bf_pieces(acc[ij])
                cols = pl.ds(pl.multiple_of(ij * elems + first, 128), 128)
                gmode[pl.ds(m * 16, 16), cols] = hi
                gmode[pl.ds(modes + m * 16, 16), cols] = hi
                gmode[pl.ds(2 * modes + m * 16, 16), cols] = lo
        return carry

    lax.fori_loop(0, elems // 128, mode_gradient, 0)

    amp_hi, amp_lo = bf_pieces(amp_ref[...].T)
    amp3 = jnp.concatenate([amp_hi, amp_lo, amp_hi], axis=1)

    piola[...] = jnp.dot(amp3, gmode[...], preferred_element_type=F32)

    def stress_rows(r, carry):
        part = pl.ds(pl.multiple_of(r * 8, 8), 8)

        def stress_cols(e, keep):
            first = pl.multiple_of(e * 128, 128)
            lanes = pl.ds(first, 128)
            at = [pl.ds(pl.multiple_of(ij * elems + first, 128), 128) for ij in range(9)]
            g = [[piola[part, at[3 * i + j]] for j in range(3)] for i in range(3)]
            lam, mu = lame_ref[0:1, lanes], lame_ref[1:2, lanes]
            twice = [[None] * 3 for _ in range(3)]
            for i in range(3):
                for j in range(i, 3):
                    quad = g[0][i] * g[0][j] + g[1][i] * g[1][j] + g[2][i] * g[2][j]
                    twice[i][j] = twice[j][i] = g[i][j] + g[j][i] + quad
            trace = (twice[0][0] + twice[1][1] + twice[2][2]) * (0.5 * lam)
            s = [[None] * 3 for _ in range(3)]
            for i in range(3):
                for j in range(i, 3):
                    v = mu * twice[i][j]
                    s[i][j] = s[j][i] = v + trace if i == j else v
            for i in range(3):
                for j in range(3):
                    p = s[i][j] + g[i][0] * s[0][j] + g[i][1] * s[1][j] + g[i][2] * s[2][j]
                    piola[part, at[3 * i + j]] = p
            return keep

        return lax.fori_loop(0, elems // 128, stress_cols, carry)

    lax.fori_loop(0, combos // 8, stress_rows, 0)

    both = jnp.concatenate(bf_pieces(piola[...]), axis=0)
    acc = lax.dot_general(
        gmode[modes : 3 * modes, :], both, NT, preferred_element_type=F32
    )
    acc = acc[:modes] + acc[modes:]
    acc = acc[:, :combos] + acc[:, combos:]
    half = modes // 2
    mine[0] = jnp.concatenate([acc[:half], acc[half:]], axis=1)

    def send_stage(s):
        copies = []
        for r, other in enumerate(groups[s]):
            copies.append(
                pltpu.make_async_remote_copy(
                    src_ref=mine.at[s], dst_ref=theirs.at[s, me[s]],
                    send_sem=as_sem.at[s, r], recv_sem=ar_sem.at[s, r],
                    device_id=other, device_id_type=MESH,
                )
            )
            copies[-1].start()
        return copies

    def end_stage(s, copies):
        theirs[s, me[s]] = mine[s]
        for copy in copies:
            copy.wait()
        total = theirs[s, 0]
        for q in range(1, 8):
            total = total + theirs[s, q]
        return total

    stage0 = send_stage(0)

    def corner_forces(e, carry):
        first = pl.multiple_of(e * 128, 128)
        lanes = pl.ds(first, 128)
        for q in range(combos // 32):
            part = pl.ds(q * 32, 32)
            for i in range(3):
                p = [
                    piola[part, pl.ds(pl.multiple_of((3 * i + j) * elems + first, 128), 128)]
                    for j in range(3)
                ]
                for a in range(8):
                    f = (
                        p[0] * grads_ref[0, pl.ds(a, 1), lanes]
                        + p[1] * grads_ref[1, pl.ds(a, 1), lanes]
                        + p[2] * grads_ref[2, pl.ds(a, 1), lanes]
                    )
                    cols = pl.ds(pl.multiple_of(a * elems + first, 128), 128)
                    for t, piece in enumerate(bf_pieces(f)):
                        forces[pl.ds(t * frows + i * combos + q * 32, 32), cols] = piece
        return carry

    lax.fori_loop(0, elems // 128, corner_forces, 0)

    def scatter(first, width):
        for a in range(8):
            near = (conn_ref[a : a + 1, :] - first).astype(jnp.int16)
            slots = lax.broadcasted_iota(jnp.int16, (width, elems), 0)
            cols = pl.ds(a * elems, elems)
            hot_block[0:width, cols] = jnp.where(slots == near, jnp.ones((), BF), jnp.zeros((), BF))
        r = lax.dot_general(forces[...], hot_block[0:width, :], NT, preferred_element_type=F32)
        return r[:frows] + r[frows:]

    backward = []

    def send_back(j, src, dst):
        backward.append(
            pltpu.make_async_remote_copy(
                src_ref=src, dst_ref=dst, send_sem=bs_sem.at[j], recv_sem=br_sem.at[j],
                device_id=halo_to[j], device_id_type=MESH,
            )
        )
        backward[-1].start()

    bk_dom[0] = scatter(nodes, wd)
    send_back(0, bk_dom.at[0], ret_dom.at[1])
    bk_dom[1] = scatter(nodes + wd, wd)
    send_back(1, bk_dom.at[1], ret_dom.at[0])
    mine[1] = end_stage(0, stage0)
    stage1 = send_stage(1)
    both = scatter(nodes + 2 * wd, 2 * ws)
    bk_sec[0] = both[:, :ws]
    bk_sec[1] = both[:, ws:]
    send_back(2, bk_sec.at[0], ret_sec.at[1])
    send_back(3, bk_sec.at[1], ret_sec.at[0])

    def own_block(b, carry):
        first = pl.multiple_of(b * 256, 256)
        out_ref[:, pl.ds(first, 256)] = scatter(first, 256)
        return carry

    blocks = nodes // 256
    lax.fori_loop(0, blocks // 2, own_block, 0)
    mine[2] = end_stage(1, stage1)
    stage2 = send_stage(2)
    lax.fori_loop(blocks // 2, blocks, own_block, 0)
    total = end_stage(2, stage2) * scale
    modal_ref[0:half, :] = total[:, :combos]
    modal_ref[half:modes, :] = total[:, combos:]

    for copy in backward:
        copy.wait()
    returned = jnp.concatenate(
        [ret_dom[0] * has_lo, ret_dom[1] * has_hi, ret_sec[0], ret_sec[1]], axis=1
    )
    r = lax.dot_general(
        jnp.concatenate(bf_pieces(returned), axis=0), hot_send[...], NT, preferred_element_type=F32
    )
    out_ref[...] = out_ref[...] + (r[:frows] + r[frows:])


def local(amplitudes, mode_shapes, shape_grads, lame_params, connectivity, dom_sends, sector_sends):
    modes, _, nodes = mode_shapes.shape
    combos = amplitudes.shape[0]
    elems = connectivity.shape[1]
    wd, ws = dom_sends.shape[1], sector_sends.shape[1]
    rows, frows, halo = 3 * modes, 3 * combos, 2 * wd + 2 * ws
    all_nodes = nodes * lax.axis_size("sector") * lax.axis_size("dom")
    vmem = pl.BlockSpec(memory_space=pltpu.VMEM)
    dma = pltpu.SemaphoreType.DMA
    nodal, modal = pl.pallas_call(
        functools.partial(kernel, 1.0 / math.sqrt(3.0 * all_nodes)),
        out_shape=(
            jax.ShapeDtypeStruct((frows, nodes), F32),
            jax.ShapeDtypeStruct((modes, combos), F32),
        ),
        in_specs=[pl.BlockSpec(memory_space=pltpu.HBM)] * 7,
        out_specs=(vmem, vmem),
        scratch_shapes=[
            pltpu.VMEM((modes, combos), F32),
            pltpu.VMEM((rows, nodes), F32),
            pltpu.VMEM((3, 8, elems), F32),
            pltpu.VMEM((2, elems), F32),
            pltpu.VMEM((8, elems), jnp.int32),
            pltpu.VMEM((2, wd), jnp.int32),
            pltpu.VMEM((2, ws), jnp.int32),
            pltpu.VMEM((2, nodes, elems), F8),
            pltpu.VMEM((nodes, halo), BF),
            pltpu.VMEM((256, 8 * elems), BF),
            pltpu.VMEM((3 * rows, nodes), F8),
            pltpu.VMEM((3 * rows, halo), F8),
            pltpu.VMEM((rows, 8 * elems), F32),
            pltpu.VMEM((3 * modes, 9 * elems), BF),
            pltpu.VMEM((combos, 9 * elems), F32),
            pltpu.VMEM((2 * frows, 8 * elems), BF),
            pltpu.VMEM((2, rows, wd), F32),
            pltpu.VMEM((2, rows, ws), F32),
            pltpu.VMEM((2, rows, wd), F32),
            pltpu.VMEM((2, rows, ws), F32),
            pltpu.VMEM((2, frows, wd), F32),
            pltpu.VMEM((2, frows, ws), F32),
            pltpu.VMEM((2, frows, wd), F32),
            pltpu.VMEM((2, frows, ws), F32),
            pltpu.VMEM((3, modes // 2, 2 * combos), F32),
            pltpu.VMEM((3, 8, modes // 2, 2 * combos), F32),
            dma((7,)), dma((4,)), dma((4,)), dma((4,)), dma((4,)), dma((3, 7)), dma((3, 7)),
        ],
        compiler_params=pltpu.CompilerParams(
            collective_id=0, has_side_effects=True, vmem_limit_bytes=36 << 20
        ),
    )(
        *(
            pltpu.with_memory_space_constraint(x, pltpu.HBM)
            for x in (
                amplitudes.T,
                mode_shapes.transpose(1, 0, 2).reshape(rows, nodes),
                shape_grads.transpose(1, 0, 2),
                lame_params,
                connectivity,
                dom_sends,
                sector_sends,
            )
        )
    )
    return nodal.reshape(3, combos, nodes).transpose(1, 0, 2), modal.T


def solution(mesh):
    placed = (
        P(),
        P(None, None, ("sector", "dom")),
        P(None, None, ("sector", "dom")),
        P(None, ("sector", "dom")),
        P(None, ("sector", "dom")),
        P(None, ("sector", "dom")),
        P(None, ("sector", "dom")),
    )
    return jax.shard_map(
        local,
        mesh=mesh,
        in_specs=placed,
        out_specs=(P(None, None, ("sector", "dom")), P()),
        check_vma=False,
    )
```
